32 devices in a mesh: grp: 2 (over y), seq: 4 (over z), ch: 2 (over x), sub: 2 (over core).
Axes of the slice: x: 2, y: 2, z: 4, core: 2. Of those that a mesh axis runs over, the one named last changes fastest.
Arguments:
- token_ids: int32 [2048], P(('grp', 'seq')), parts along dimension 0, may hold values from 0 to 511
- residual_in: bfloat16 [2048, 4096], P(('grp', 'seq'), ('ch', 'sub')), parts along dimension 0, may hold values from -6 to 6
- embedding: bfloat16 [512, 4096], P(None, ('ch', 'sub')), may hold values from -6 to 6
- in_weight: bfloat16 [4096, 3, 2048], P('seq', None, ('ch', 'sub')), may hold values from -0.09375 to 0.09375
- short_filter: float32 [3, 3, 2048], P(None, None, ('ch', 'sub')), may hold values from -3 to 3
- decay_rate: float32 [16, 2048], P(None, ('ch', 'sub')), may hold values from 1e-05 to 0.05
- residue: float32 [16, 2048], P(None, ('ch', 'sub')), may hold values from -0.24 to 0.24
- skip: float32 [2048], P(('ch', 'sub')), may hold values from -4 to 4
Outputs:
- mixed_out: bfloat16 [2048, 2048], P(('grp', 'seq'), ('ch', 'sub')), parts along dimension 0
The draws below stay inside these ranges and needn't reach their ends.
There are 2 independent parts, one for each index of `grp`. The reference program is written for one: setup_inputs(seed, part) draws one part's arguments, and reference() takes and returns one part's arrays. A program takes and returns all parts, laid end to end along the dimension named above; an argument that names none is the same for every part. Nothing has to cross between parts.
All inputs are finite; a program needn't handle non-finite values.
Results may differ from the reference program's by a relative error of at most 0.0095.
Values may be sent and summed in bfloat16 or wider, within the bound.
A program may use at most 64 MiB of HBM per device.

```python
import math
import jax
import jax.numpy as jnp
import numpy as np
from jax import lax

D = 4096
V = 512
C = 2048
MODES = 16
SHORT = 3
TOKENS = 1024


def modal_rates(key):
    sample = jax.random.uniform(jax.random.fold_in(key, 17), (MODES, C), jnp.float32)
    lower_end = 0.0001
    upper_end = 0.05
    return jnp.exp(jnp.log(lower_end) + sample * (jnp.log(upper_end) - jnp.log(lower_end)))


def draw_decay_rate(key, part):
    return modal_rates(key)


def draw_residue(key, part):
    rates = modal_rates(key)
    normal_part = jax.random.truncated_normal(jax.random.fold_in(key, 29), -3.0, 3.0, (MODES, C), jnp.float32)
    return normal_part * jnp.sqrt(2.0 * rates / 16.0)


def plant(drawn, rng, least, high):
    index_at = [jax.random.randint(jax.random.fold_in(rng, axis), (), 0, length) for axis, length in enumerate(drawn.shape)]
    main_axis = drawn.shape.index(max(drawn.shape))
    neighbour = index_at[:main_axis] + [(index_at[main_axis] + 1) % drawn.shape[main_axis]] + index_at[main_axis + 1:]
    return drawn.at[tuple(index_at)].set(least).at[tuple(neighbour)].set(high)


def level_of(own_key, extent, shards, least, high):
    factor_of, own = 1.0, jax.random.fold_in(own_key, 6)
    for dim, shards_of in shards:
        draws = jnp.exp(jax.random.uniform(jax.random.fold_in(own, dim), (shards_of,), jnp.float32, least / len(shards), high / len(shards)))
        factor_of = factor_of * jnp.repeat(draws, extent[dim] // shards_of).reshape([-1 if axis == dim else 1 for axis in range(len(extent))])
    return factor_of


def rank_table(number_of, lean):
    weights = [(1 << 20) // math.isqrt(standing ** lean) + 1 for standing in range(1, number_of + 1)]
    spread = 1 + sum(weights) // (1 << 30)
    return np.cumsum(np.array([max(1, weight // spread) for weight in weights]))


def skewed_ids(rng, dims, amount, skew):
    grid = rank_table(amount, skew)
    pick = jax.random.randint(jax.random.fold_in(rng, 1), dims, 0, int(grid[amount - 1]))
    standing = jnp.searchsorted(jnp.asarray(grid, jnp.int32), pick, side="right")
    return jax.random.permutation(jax.random.fold_in(rng, 2), amount)[standing].astype(jnp.int32)


def noise(rng, extent, deviation, most, pieces=(), held_as=jnp.bfloat16):
    result = deviation * jax.random.normal(rng, extent, jnp.float32)
    if pieces:
        result = result * level_of(rng, extent, pieces, -0.22, 0.18)
    return jnp.clip(result, -most, most).astype(held_as)


def setup_inputs(seed: int = 0, part: int = 0) -> dict:
    key_of = jax.random.split(jax.random.key(seed), 9)
    own_keys = jax.random.split(jax.random.fold_in(key_of[8], part), 9)
    token_ids = plant(skewed_ids(own_keys[0], (TOKENS,), V, 2), jax.random.fold_in(own_keys[0], 3), 0, V - 1).astype(jnp.int32)
    residual_in = noise(own_keys[1], (TOKENS, D), 1.0, 6.0, ((0, 4), (1, 4)))
    embedding = noise(key_of[2], (V, D), 1.0, 6.0, ((1, 4),))
    in_weight = noise(key_of[3], (D, 3, C), D ** -0.5, 0.09375, ((0, 4), (2, 4)))
    short_filter = noise(key_of[4], (SHORT, 3, C), 0.5, 3.0, ((2, 4),), jnp.float32)
    decay_rate = draw_decay_rate(jax.random.fold_in(key_of[8], 71), part)
    residue = draw_residue(jax.random.fold_in(key_of[8], 71), part)
    skip = noise(key_of[7], (C,), 1.0, 4.0, ((0, 4),), jnp.float32)
    return {"token_ids": token_ids, "residual_in": residual_in, "embedding": embedding, "in_weight": in_weight, "short_filter": short_filter, "decay_rate": decay_rate, "residue": residue, "skip": skip}


def reference(token_ids, residual_in, embedding, in_weight, short_filter, decay_rate, residue, skip):
    embedded = jnp.take(embedding, token_ids, axis=0).astype(jnp.float32)
    inputs = (residual_in.astype(jnp.float32) + embedded).astype(jnp.bfloat16)
    projected = jnp.dot(inputs, in_weight.reshape(D, 3 * C), preferred_element_type=jnp.float32)
    projected = lax.optimization_barrier(projected.astype(jnp.bfloat16)).reshape(TOKENS, 3, C).astype(jnp.float32)
    zero_rows = jnp.zeros((2, 3, C), jnp.float32)
    padded = jnp.concatenate([zero_rows, projected], axis=0)
    mixed_in = short_filter[0] * padded[2:] + short_filter[1] * padded[1:-1] + short_filter[2] * padded[:-2]
    query_gate = mixed_in[:, 0]
    product = lax.optimization_barrier((mixed_in[:, 1] * mixed_in[:, 2]).astype(jnp.bfloat16)).astype(jnp.float32)
    delay_steps = jnp.arange(TOKENS).astype(jnp.float32)[:, None]
    filter_taps = jnp.zeros((TOKENS, C), jnp.float32)
    for mode_index in range(MODES):
        filter_taps = filter_taps + residue[mode_index] * jnp.exp(-decay_rate[mode_index] * delay_steps)
    spec_input = jnp.fft.rfft(product, n=2 * TOKENS, axis=0)
    spec_filter = jnp.fft.rfft(filter_taps, n=2 * TOKENS, axis=0)
    conv_out = jnp.fft.irfft(spec_input * spec_filter, n=2 * TOKENS, axis=0)[:TOKENS].astype(jnp.float32)
    return (query_gate * (conv_out + skip * product)).astype(jnp.bfloat16)
```

```python
import functools

import jax
import jax.numpy as jnp
from jax import lax
from jax.experimental import pallas as pl
from jax.experimental.pallas import tpu as pltpu
from jax.sharding import PartitionSpec as P

PRECISE = lax.Precision.HIGHEST
TWO_PI = 6.283185307179586


def shifted(x, axis, by):
    peers = lax.axis_size(axis)
    pairs = [(i, i + by) for i in range(peers) if 0 <= i + by < peers]
    return lax.ppermute(x, axis, pairs)


def swapped(value, axis, apart):
    mask = 2**apart
    pairs = [(source, source ^ mask) for source in range(lax.axis_size(axis))]
    return lax.ppermute(value, axis, pairs)


def reversed_bits(number, bit_count):
    result = jnp.zeros_like(number)
    for section_bit in range(bit_count):
        result = result + (number >> section_bit & 1) * (1 << bit_count - 1 - section_bit)
    return result


def angle_table(left_idx, right_idx, period):
    wrapped = left_idx[:, None] * right_idx[None, :] % period
    return TWO_PI * wrapped.astype(jnp.float32) / period


def complex_mix(mat_re, mat_im, data_re, data_im):
    real_part = jnp.einsum("kr,rjc->kjc", mat_re, data_re, precision=PRECISE) - jnp.einsum(
        "kr,rjc->kjc", mat_im, data_im, precision=PRECISE
    )
    imag_part = jnp.einsum("kr,rjc->kjc", mat_re, data_im, precision=PRECISE) + jnp.einsum(
        "kr,rjc->kjc", mat_im, data_re, precision=PRECISE
    )
    return (real_part, imag_part)


def complex_dot(mat_re, mat_im, data_re, data_im):
    real_part = jnp.dot(mat_re, data_re, precision=PRECISE) - jnp.dot(
        mat_im, data_im, precision=PRECISE
    )
    imag_part = jnp.dot(mat_re, data_im, precision=PRECISE) + jnp.dot(
        mat_im, data_re, precision=PRECISE
    )
    return (real_part, imag_part)


def shards(token_ids, residual_in, embedding, in_weight, short_filter, decay_rate, residue, skip):
    tok_rows = residual_in.shape[0]
    vocab_size = embedding.shape[0]
    channels = skip.shape[0]
    seq_parts = lax.axis_size("seq")
    bit_count = seq_parts.bit_length() - 1
    my_index = lax.axis_index("seq")
    length = tok_rows * seq_parts
    padded_len = 2 * length
    group_rows = tok_rows // seq_parts
    onehot = (token_ids[:, None] == jnp.arange(vocab_size, dtype=jnp.int32)[None, :]).astype(
        jnp.bfloat16
    )
    embedded = jnp.dot(onehot, embedding, preferred_element_type=jnp.float32)
    inputs = (residual_in.astype(jnp.float32) + embedded).astype(jnp.bfloat16)
    features = lax.all_gather(inputs, ("ch", "sub"), axis=1, tiled=True)
    piece_rows = lax.all_gather(in_weight, "seq", axis=0, tiled=True)
    flat_piece = piece_rows.reshape(piece_rows.shape[0], 3 * channels)
    projected = jnp.dot(features, flat_piece, preferred_element_type=jnp.float32)
    projected = projected.astype(jnp.bfloat16).reshape(tok_rows, 3, channels)
    rim_rows = shifted(projected[tok_rows - 2 :], "seq", 1)
    extended = jnp.concatenate([rim_rows, projected], axis=0).astype(jnp.float32)
    mixed_in = (
        short_filter[0] * extended[2:]
        + short_filter[1] * extended[1:-1]
        + short_filter[2] * extended[:-2]
    )
    query_gate = mixed_in[:, 0]
    product = (mixed_in[:, 1] * mixed_in[:, 2]).astype(jnp.bfloat16)
    local_pos = jnp.arange(tok_rows, dtype=jnp.int32)
    sources = jnp.arange(seq_parts, dtype=jnp.int32)
    within_rows = my_index * group_rows + jnp.arange(group_rows, dtype=jnp.int32)
    block_pos = sources[:, None] * tok_rows + within_rows[None, :]
    block_angle = TWO_PI * block_pos.astype(jnp.float32) / padded_len
    pos_angle = TWO_PI * (my_index * tok_rows + local_pos).astype(jnp.float32) / padded_len
    values = product.astype(jnp.float32)
    state_re = jnp.concatenate([values, values * jnp.cos(pos_angle)[:, None]], -1)
    state_im = jnp.concatenate([jnp.zeros_like(values), -values * jnp.sin(pos_angle)[:, None]], -1)
    state_now = jnp.stack([state_re, state_im])
    for section_bit in range(bit_count - 1, -1, -1):
        half_span = 1 << section_bit
        partner = swapped(state_now.astype(jnp.bfloat16), "seq", section_bit).astype(
            state_now.dtype
        )
        upper_half = my_index >> section_bit & 1 == 1
        phase_now = TWO_PI * (my_index % half_span).astype(jnp.float32) / (2 * half_span)
        difference = partner - state_now
        rot_re = difference[0] * jnp.cos(phase_now) + difference[1] * jnp.sin(phase_now)
        rot_im = difference[1] * jnp.cos(phase_now) - difference[0] * jnp.sin(phase_now)
        state_now = jnp.where(upper_half, jnp.stack([rot_re, rot_im]), state_now + partner)
    own_freq = reversed_bits(my_index, bit_count)
    holders = reversed_bits(sources, bit_count)
    twist_angle = TWO_PI * (local_pos * own_freq % length).astype(jnp.float32) / length
    twist_re = jnp.cos(twist_angle)[:, None]
    twist_im = -jnp.sin(twist_angle)[:, None]
    spec_re = state_now[0] * twist_re - state_now[1] * twist_im
    spec_im = state_now[0] * twist_im + state_now[1] * twist_re
    kernel_table = angle_table(local_pos, local_pos, tok_rows)
    dft_re = jnp.cos(kernel_table)
    dft_im = -jnp.sin(kernel_table)
    spec_re, spec_im = complex_dot(dft_re, dft_im, spec_re, spec_im)
    parity = (jnp.arange(2 * channels, dtype=jnp.int32) >= channels).astype(jnp.int32)
    full_freq = 2 * (own_freq + seq_parts * local_pos)[:, None] + parity[None, :]
    freq_angle = TWO_PI * full_freq.astype(jnp.float32) / padded_len
    half_sine = jnp.sin(0.5 * freq_angle)
    sine_full = jnp.sin(freq_angle)
    sign_flip = 1.0 - 2.0 * parity.astype(jnp.float32)
    rates_both = jnp.concatenate([decay_rate, decay_rate], -1)
    residues_both = jnp.concatenate([residue, residue], -1)
    filt_re = jnp.zeros_like(spec_re)
    filt_im = jnp.zeros_like(spec_re)
    for mode_index in range(rates_both.shape[0]):
        rate_now = rates_both[mode_index]
        decay_now = jnp.exp(-rate_now)
        numerator = residues_both[mode_index] * (1.0 - sign_flip * jnp.exp(-rate_now * length))
        denom_re = -jnp.expm1(-rate_now) + 2.0 * decay_now * half_sine * half_sine
        denom_im = decay_now * sine_full
        scaled = numerator / (denom_re * denom_re + denom_im * denom_im)
        filt_re = filt_re + scaled * denom_re
        filt_im = filt_im - scaled * denom_im
    prod_re = spec_re * filt_re - spec_im * filt_im
    prod_im = spec_re * filt_im + spec_im * filt_re
    inv_re, inv_im = complex_dot(dft_re, -dft_im, prod_re, prod_im)
    back_re = inv_re * twist_re + inv_im * twist_im
    back_im = inv_im * twist_re - inv_re * twist_im
    returned = lax.all_to_all(
        jnp.stack([back_re, back_im]).reshape(2, 1, tok_rows, 2 * channels).astype(jnp.bfloat16),
        "seq",
        split_axis=2,
        concat_axis=1,
        tiled=True,
    ).astype(jnp.float32)
    inverse_angle = angle_table(sources, holders, seq_parts)
    block_re, block_im = complex_mix(
        jnp.cos(inverse_angle), jnp.sin(inverse_angle), returned[0], returned[1]
    )
    conv_blocks = (
        block_re[..., :channels]
        + jnp.cos(block_angle)[:, :, None] * block_re[..., channels:]
        - jnp.sin(block_angle)[:, :, None] * block_im[..., channels:]
    )
    conv_blocks = conv_blocks / padded_len
    conv_rows = lax.all_to_all(conv_blocks, "seq", split_axis=0, concat_axis=1, tiled=True)[0]
    mixed_out = (query_gate * (conv_rows + skip * product.astype(jnp.float32))).astype(jnp.bfloat16)
    return mixed_out


MESH = pl.DeviceIdType.MESH
PIECES = 4
AHEAD = 3
SEGMENTS = 8


def fused_block(
    x_ref, w_ref, taps_ref, rate_ref, residue_ref, skip_ref, out_ref,
    held, weights, stage, outbox, inbox, edge, halo, proj, values, conv, enter, ends, states,
    load_sem, wide_send, wide_recv, weight_send, weight_recv, x_send, x_recv, via_send, via_recv,
    box_send, box_recv, edge_send, edge_recv, end_send, end_recv,
):
    y = lax.axis_index("grp")
    z = lax.axis_index("seq")
    ch = lax.axis_index("ch")
    sub = lax.axis_index("sub")
    rows = x_ref.shape[0]
    width = x_ref.shape[1]
    parts, tall = 4, width // 2
    units, lanes = weights.shape[1], weights.shape[3]
    blocks = units // 3
    pairs = 2 * blocks
    modes = rate_ref.shape[0]
    taps_count = taps_ref.shape[0]
    span = rows // SEGMENTS
    f32, bf16 = jnp.float32, jnp.bfloat16

    side = z // 2
    near = 1 + side
    outer = 3 * side
    far_near = 2 - side
    far_outer = 3 - outer
    is_outer = z == outer
    is_inner = z == near
    mine = lax.rem(z, 2)
    across = {"ch": 1 - ch}
    sibling = {"sub": 1 - sub}
    other_group = {"grp": 1 - y}

    def remote(src, dst, send, recv, device):
        return pltpu.make_async_remote_copy(
            src_ref=src, dst_ref=dst, send_sem=send, recv_sem=recv, device_id=device, device_id_type=MESH
        )

    def place(u):
        pair = u < pairs
        return jnp.where(pair, 1 + lax.rem(u, 2), 0), jnp.where(pair, u // 2, u - pairs)

    def load(u):
        g, h = (1 + u % 2, u // 2) if u < pairs else (0, u - pairs)
        return pltpu.make_async_copy(
            w_ref.at[g, :, pl.ds(h * lanes, lanes)], weights.at[mine, u], load_sem.at[u]
        )

    def loaded(u):
        pltpu.make_async_copy(w_ref.at[0, :, pl.ds(0, lanes)], weights.at[mine, u], load_sem.at[u]).wait()

    for u in range(units):
        load(u).start()
    halo[...] = jnp.zeros_like(halo)
    states[...] = jnp.zeros_like(states)

    barrier = pltpu.get_barrier_semaphore()
    for device in (across, sibling, other_group):
        pl.semaphore_signal(barrier, inc=1, device_id=device, device_id_type=MESH)
    for apart in range(1, parts):
        pl.semaphore_signal(barrier, inc=1, device_id={"seq": lax.rem(z + apart, parts)}, device_id_type=MESH)
    pl.semaphore_wait(barrier, 3 + parts - 1)

    share = pl.ds(pl.multiple_of(y * tall, tall), tall)

    def weight_up(u):
        at = weights.at[mine, u, share]
        return remote(at, at, weight_send.at[u], weight_recv.at[u], {"seq": near})

    def weight_wide(u):
        at = weights.at[1 - mine, u, share]
        return remote(at, at, wide_send.at[u], wide_recv.at[u], other_group)

    def weight_share(u):
        at = weights.at[1 - mine, u, share]
        remote(at, at, weight_send.at[u], weight_recv.at[u], other_group).wait_recv()
        weight_wide(u).start()

    step = rows // PIECES
    direct = PIECES // 2

    def piece(p):
        return pl.ds(p * step, step) if isinstance(p, int) else pl.ds(pl.multiple_of(p * step, step), step)

    def target(c):
        f = 2 * c + sub
        return jnp.where((f == z) & is_outer, z, 1 + c)

    goal = target(ch)
    relay_goal = target(1 - ch)
    stays = goal == z
    relay_stays = relay_goal == z

    def own_direct(p):
        return remote(x_ref.at[piece(p)], held.at[z, sub, piece(p)], x_send.at[0, p], x_recv.at[z, sub, p], {"seq": goal})

    def own_local(p):
        return pltpu.make_async_copy(x_ref.at[piece(p)], held.at[z, sub, piece(p)], x_recv.at[z, sub, p])

    def own_across(p):
        return remote(x_ref.at[piece(p)], held.at[z, sub, piece(p)], x_send.at[0, p], x_recv.at[z, sub, p], across)

    def own_via(p):
        return remote(x_ref.at[piece(p)], stage.at[p - direct], x_send.at[0, p], via_recv.at[p - direct], across)

    def relay(p):
        return remote(
            stage.at[p - direct], held.at[z, sub, piece(p)], via_send.at[p - direct], x_recv.at[z, sub, p],
            {"seq": relay_goal},
        )

    def send_via():
        @pl.when(stays)
        def _():
            for p in range(direct, PIECES):
                own_across(p).start()

        @pl.when(jnp.logical_not(stays))
        def _():
            for p in range(direct, PIECES):
                own_via(p).start()

    def send_direct():
        @pl.when(stays)
        def _():
            for p in range(direct):
                own_local(p).start()

        @pl.when(jnp.logical_not(stays))
        def _():
            for p in range(direct):
                own_direct(p).start()

    def send_relay():
        @pl.when(jnp.logical_not(relay_stays))
        def _():
            for p in range(direct, PIECES):
                own_via(p).wait_recv()
                relay(p).start()

    at_home = ch == side
    first = jnp.where(at_home, 0, direct)
    second = direct - first

    def arrived(t, s, p):
        at = held.at[t, s, piece(p)]
        remote(at, at, x_send.at[1, p], x_recv.at[t, s, p], across).wait_recv()

    def to_across(t, p):
        at = held.at[t, sub, piece(p)]
        return remote(at, at, x_send.at[1 + t, p], x_recv.at[t, sub, p], across)

    def to_sibling(t, p):
        at = held.at[t, sub, piece(p)]
        return remote(at, at, x_send.at[1 + parts + t, p], x_recv.at[t, sub, p], sibling)

    def primary(t):
        for n in range(direct):
            p = first + n
            arrived(t, sub, p)
            to_across(t, p).start()
            to_sibling(t, p).start()

    def secondary(t):
        for n in range(PIECES - direct):
            p = second + n
            arrived(t, sub, p)
            to_sibling(t, p).start()

    def from_sibling(t):
        for p in range(PIECES):
            arrived(t, 1 - sub, p)

    def outgoing(kind, u, device, there):
        return remote(
            outbox.at[kind, u], inbox.at[there, u], box_send.at[kind, u], box_recv.at[there, u], device
        )

    def both(t, u):
        return jnp.dot(held[t, 0], weights[0, u], preferred_element_type=f32) + jnp.dot(
            held[t, 1], weights[1, u], preferred_element_type=f32
        )

    def one(t, u):
        return jnp.dot(held[t, mine], weights[mine, u], preferred_element_type=f32)

    def received(kind, u):
        outgoing(kind, u, across, kind).wait_recv()
        return inbox[kind, u].astype(f32)

    def far(kind, t, u):
        outbox[kind, u] = both(t, u).astype(bf16)
        outgoing(kind, u, {"seq": far_near}, kind).start()

    def weights_ready(u):
        loaded(u)
        at = weights.at[1 - mine, u, share]
        remote(at, at, wide_send.at[u], wide_recv.at[u], other_group).wait_recv()

    def to_outer(u):
        acc = one(outer, u)
        outbox[2, u] = (acc + received(1, u)).astype(bf16)
        outgoing(2, u, {"seq": outer}, 0).start()

    def edge_copy(u):
        return remote(edge.at[u], halo.at[u], edge_send.at[u], edge_recv.at[u], {"seq": z + 1})

    def finished(acc, u):
        total = (acc + received(0, u)).astype(bf16)
        proj[u, SEGMENTS:, :] = total.astype(f32)

        @pl.when(z < parts - 1)
        def _():
            edge[u] = total[rows - 16 :]
            edge_copy(u).start()

    def lanes_at(h):
        return pl.ds(pl.multiple_of(h * lanes, lanes), lanes)

    def mixed(g, u, h):
        proj[u, :SEGMENTS, :] = halo[u].astype(f32)[16 - SEGMENTS :]
        acc = None
        for i in range(taps_count):
            term = taps_ref[i, g : g + 1, lanes_at(h)] * proj[u, pl.ds(SEGMENTS - i, rows), :]
            acc = term if acc is None else acc + term
        return acc

    def halo_ready(u):
        @pl.when(z > 0)
        def _():
            remote(edge.at[u], halo.at[u], edge_send.at[u], edge_recv.at[u], across).wait_recv()

    index = lax.broadcasted_iota(jnp.int32, (SEGMENTS, lanes), 0)

    def wide(row):
        return jnp.broadcast_to(row, (SEGMENTS, lanes))

    def end_copy(h, apart):
        return remote(
            ends.at[h], states.at[z, h], end_send.at[apart - 1, h], end_recv.at[z, h], {"seq": z + apart}
        )

    def local_scan(h):
        rates = rate_ref[:, lanes_at(h)]
        decay = [wide(jnp.exp(-rates[m : m + 1, :])) for m in range(modes)]
        zero = jnp.zeros((SEGMENTS, lanes), f32)

        def advance(j, state):
            now = values[h, pl.ds(j, SEGMENTS, stride=span), :]
            return tuple(v * d + now for v, d in zip(state, decay))

        state = lax.fori_loop(0, span, advance, (zero,) * modes, unroll=4)

        def down(v, by):
            return jnp.where(index >= by, pltpu.roll(v, by, 0), 0.0)

        for m in range(modes):
            carry = down(state[m], 1)
            by = 1
            while by < SEGMENTS:
                carry = carry + jnp.exp(-rates[m : m + 1, :] * (span * by)) * down(carry, by)
                by *= 2
            enter[h, m] = carry
            last = slice(SEGMENTS - 1, SEGMENTS)
            ends[h, m : m + 1, :] = jnp.exp(-rates[m : m + 1, :] * span) * carry[last] + state[m][last]
        for apart in range(1, parts):
            @pl.when(z + apart < parts)
            def _():
                end_copy(h, apart).start()

    def full_scan(h):
        rates = rate_ref[:, lanes_at(h)]
        scale = residue_ref[:, lanes_at(h)]
        for t in range(parts - 1):
            @pl.when(t < z)
            def _():
                remote(ends.at[h], states.at[t, h], end_send.at[0, h], end_recv.at[t, h], across).wait_recv()

        decay = [wide(jnp.exp(-rates[m : m + 1, :])) for m in range(modes)]
        weight = [wide(scale[m : m + 1, :]) for m in range(modes)]
        whole = jnp.exp(-rates * rows)
        start = states[0, h]
        for t in range(1, parts - 1):
            start = jnp.where(t < z, start * whole + states[t, h], start)
        steps = (index * span).astype(f32)
        begin = tuple(
            enter[h, m] + jnp.exp(-rates[m : m + 1, :] * steps) * start[m : m + 1, :] for m in range(modes)
        )
        skips = wide(skip_ref[:, lanes_at(h)])

        def advance(j, state):
            here = pl.ds(j, SEGMENTS, stride=span)
            now = values[h, here, :]
            state = tuple(v * d + now for v, d in zip(state, decay))
            terms = [v * w for v, w in zip(state, weight)] + [skips * now]
            while len(terms) > 1:
                terms = [a + b for a, b in zip(terms[::2], terms[1::2])] + terms[len(terms) // 2 * 2 :]
            conv[h, here, :] = terms[0]
            return state

        lax.fori_loop(0, span, advance, begin, unroll=4)

    def mix(u):
        halo_ready(u)
        _, h = place(u)

        @pl.when((u < pairs) & (lax.rem(u, 2) == 1))
        def _():
            product = mixed(1, u - 1, h) * mixed(2, u, h)
            values[h] = product.astype(bf16).astype(f32)
            local_scan(h)

        @pl.when(u >= pairs)
        def _():
            out_ref[:, lanes_at(h)] = (mixed(0, u, h) * conv[h]).astype(out_ref.dtype)

    @pl.when(is_outer)
    def _():
        loaded(0)
        weight_up(0).start()
        send_via()
        send_direct()
        for u in range(1, AHEAD):
            loaded(u)
            weight_up(u).start()
        send_relay()
        for u in range(AHEAD, units):
            loaded(u)
            weight_up(u).start()

        @pl.when(sub == mine)
        def _():
            primary(z)
            secondary(z)

        @pl.when(sub != mine)
        def _():
            from_sibling(z)

        @pl.loop(0, units + 1)
        def _(u):
            @pl.when(u > pairs)
            def _():
                full_scan(u - 1 - pairs)

            @pl.when(u < units)
            def _():
                finished(one(z, u), u)

            @pl.when(u > 0)
            def _():
                mix(u - 1)

    @pl.when(is_inner)
    def _():
        handles_near = sub == mine
        send_via()
        send_direct()
        send_relay()
        weight_share(0)
        primary(far_near)
        weight_share(1)
        secondary(far_near)
        primary(far_outer)
        for u in range(2, AHEAD):
            weight_share(u)
        from_sibling(far_near)

        @pl.loop(0, AHEAD)
        def _(u):
            weights_ready(u)
            far(0, far_near, u)

        secondary(far_outer)
        primary(z)
        weight_share(AHEAD)

        @pl.when(handles_near)
        def _():
            primary(outer)

        from_sibling(far_outer)
        lag = 3

        @pl.loop(0, units + lag)
        def _(i):
            @pl.when(i < units)
            def _():
                far(1, far_outer, i)

            @pl.when(i + AHEAD < units)
            def _():
                weights_ready(i + AHEAD)
                far(0, far_near, i + AHEAD)

            @pl.when(i + AHEAD + 1 < units)
            def _():
                weight_share(i + AHEAD + 1)

            @pl.when(i == 0)
            def _():
                secondary(z)

                @pl.when(handles_near)
                def _():
                    secondary(outer)

                from_sibling(z)

                @pl.when(jnp.logical_not(handles_near))
                def _():
                    from_sibling(outer)

            @pl.when((i > 0) & (i <= units))
            def _():
                to_outer(i - 1)
                finished(both(z, i - 1), i - 1)

            @pl.when((i >= pairs + lag - 1) & (i < units + lag - 1))
            def _():
                full_scan(i - pairs - lag + 1)

            @pl.when(i >= lag)
            def _():
                mix(i - lag)

    for p in range(PIECES):
        @pl.when(jnp.logical_not(stays) | (p >= direct))
        def _():
            own_direct(p).wait_send()

    @pl.when(jnp.logical_not(relay_stays))
    def _():
        for p in range(direct, PIECES):
            relay(p).wait_send()

    def sent(t):
        for n in range(direct):
            to_across(t, first + n).wait_send()
        for p in range(PIECES):
            to_sibling(t, p).wait_send()

    @pl.when(is_outer & (sub == mine))
    def _():
        sent(z)

    @pl.when(is_inner)
    def _():
        sent(far_near)
        sent(far_outer)
        sent(z)

        @pl.when(sub == mine)
        def _():
            sent(outer)

    @pl.loop(0, units)
    def _(u):
        @pl.when(is_outer)
        def _():
            weight_up(u).wait_send()

        @pl.when(is_inner)
        def _():
            weight_wide(u).wait_send()
            for kind in range(3):
                outgoing(kind, u, across, 0).wait_send()

        @pl.when(z < parts - 1)
        def _():
            remote(edge.at[u], halo.at[u], edge_send.at[u], edge_recv.at[u], across).wait_send()

    for h in range(blocks):
        for apart in range(1, parts):
            @pl.when(z + apart < parts)
            def _():
                remote(
                    ends.at[h], states.at[0, h], end_send.at[apart - 1, h], end_recv.at[0, h], across
                ).wait_send()


def fused(inputs, weight, short_filter, decay_rate, residue, skip):
    rows, width = inputs.shape
    groups, _, channels = weight.shape
    parts = 4
    modes = decay_rate.shape[0]
    lanes = 128
    blocks = channels // lanes
    units = groups * blocks
    dma = pltpu.SemaphoreType.DMA
    f32, bf16 = jnp.float32, jnp.bfloat16
    vmem = pl.BlockSpec(memory_space=pltpu.VMEM)
    return pl.pallas_call(
        fused_block,
        out_shape=jax.ShapeDtypeStruct((rows, channels), jnp.bfloat16),
        in_specs=[vmem, pl.BlockSpec(memory_space=pl.ANY)] + [vmem] * 4,
        out_specs=vmem,
        scratch_shapes=[
            pltpu.VMEM((parts, 2, rows, width), bf16),
            pltpu.VMEM((2, units, width, lanes), bf16),
            pltpu.VMEM((PIECES - PIECES // 2, rows // PIECES, width), bf16),
            pltpu.VMEM((3, units, rows, lanes), bf16),
            pltpu.VMEM((2, units, rows, lanes), bf16),
            pltpu.VMEM((units, 16, lanes), bf16),
            pltpu.VMEM((units, 16, lanes), bf16),
            pltpu.VMEM((units, rows + SEGMENTS, lanes), f32),
            pltpu.VMEM((blocks, rows, lanes), f32),
            pltpu.VMEM((blocks, rows, lanes), f32),
            pltpu.VMEM((blocks, modes, SEGMENTS, lanes), f32),
            pltpu.VMEM((blocks, modes, lanes), f32),
            pltpu.VMEM((parts - 1, blocks, modes, lanes), f32),
            dma((units,)),
            dma((units,)),
            dma((units,)),
            dma((units,)),
            dma((units,)),
            dma((1 + 2 * parts, PIECES)),
            dma((parts, 2, PIECES)),
            dma((PIECES - PIECES // 2,)),
            dma((PIECES - PIECES // 2,)),
            dma((3, units)),
            dma((2, units)),
            dma((units,)),
            dma((units,)),
            dma((parts - 1, blocks)),
            dma((parts - 1, blocks)),
        ],
        compiler_params=pltpu.CompilerParams(
            collective_id=0, has_side_effects=True, vmem_limit_bytes=60 * 2**20
        ),
    )(inputs, weight, short_filter, decay_rate, residue, skip.reshape(1, -1))


def fast_shards(token_ids, residual_in, embedding, in_weight, short_filter, decay_rate, residue, skip):
    vocab_size = embedding.shape[0]
    onehot = (token_ids[:, None] == jnp.arange(vocab_size, dtype=jnp.int32)[None, :]).astype(jnp.bfloat16)
    embedded = jnp.dot(onehot, embedding, preferred_element_type=jnp.float32)
    inputs = (residual_in.astype(jnp.float32) + embedded).astype(jnp.bfloat16)
    return fused(inputs, in_weight.transpose(1, 0, 2), short_filter, decay_rate, residue, skip)


def fits(mesh):
    shape = mesh.shape
    return shape["seq"] == 4 and shape["grp"] == 2 and shape["ch"] == 2 and shape["sub"] == 2


def solution(mesh):
    return jax.shard_map(
        fast_shards if fits(mesh) else shards,
        mesh=mesh,
        in_specs=(
            P(("grp", "seq")),
            P(("grp", "seq"), ("ch", "sub")),
            P(None, ("ch", "sub")),
            P("seq", None, ("ch", "sub")),
            P(None, None, ("ch", "sub")),
            P(None, ("ch", "sub")),
            P(None, ("ch", "sub")),
            P(("ch", "sub")),
        ),
        out_specs=P(("grp", "seq"), ("ch", "sub")),
        check_vma=False,
    )
```

```python
import functools

import jax
import jax.numpy as jnp
from jax import lax
from jax.experimental import pallas as pl
from jax.experimental.pallas import tpu as pltpu
from jax.sharding import PartitionSpec as P

PRECISE = lax.Precision.HIGHEST
TWO_PI = 6.283185307179586


def shifted(x, axis, by):
    peers = lax.axis_size(axis)
    pairs = [(i, i + by) for i in range(peers) if 0 <= i + by < peers]
    return lax.ppermute(x, axis, pairs)


def swapped(value, axis, apart):
    mask = 2**apart
    pairs = [(source, source ^ mask) for source in range(lax.axis_size(axis))]
    return lax.ppermute(value, axis, pairs)


def reversed_bits(number, bit_count):
    result = jnp.zeros_like(number)
    for section_bit in range(bit_count):
        result = result + (number >> section_bit & 1) * (1 << bit_count - 1 - section_bit)
    return result


def angle_table(left_idx, right_idx, period):
    wrapped = left_idx[:, None] * right_idx[None, :] % period
    return TWO_PI * wrapped.astype(jnp.float32) / period


def complex_mix(mat_re, mat_im, data_re, data_im):
    real_part = jnp.einsum("kr,rjc->kjc", mat_re, data_re, precision=PRECISE) - jnp.einsum(
        "kr,rjc->kjc", mat_im, data_im, precision=PRECISE
    )
    imag_part = jnp.einsum("kr,rjc->kjc", mat_re, data_im, precision=PRECISE) + jnp.einsum(
        "kr,rjc->kjc", mat_im, data_re, precision=PRECISE
    )
    return (real_part, imag_part)


def complex_dot(mat_re, mat_im, data_re, data_im):
    real_part = jnp.dot(mat_re, data_re, precision=PRECISE) - jnp.dot(
        mat_im, data_im, precision=PRECISE
    )
    imag_part = jnp.dot(mat_re, data_im, precision=PRECISE) + jnp.dot(
        mat_im, data_re, precision=PRECISE
    )
    return (real_part, imag_part)


def shards(token_ids, residual_in, embedding, in_weight, short_filter, decay_rate, residue, skip):
    tok_rows = residual_in.shape[0]
    vocab_size = embedding.shape[0]
    channels = skip.shape[0]
    seq_parts = lax.axis_size("seq")
    bit_count = seq_parts.bit_length() - 1
    my_index = lax.axis_index("seq")
    length = tok_rows * seq_parts
    padded_len = 2 * length
    group_rows = tok_rows // seq_parts
    onehot = (token_ids[:, None] == jnp.arange(vocab_size, dtype=jnp.int32)[None, :]).astype(
        jnp.bfloat16
    )
    embedded = jnp.dot(onehot, embedding, preferred_element_type=jnp.float32)
    inputs = (residual_in.astype(jnp.float32) + embedded).astype(jnp.bfloat16)
    features = lax.all_gather(inputs, ("ch", "sub"), axis=1, tiled=True)
    piece_rows = lax.all_gather(in_weight, "seq", axis=0, tiled=True)
    flat_piece = piece_rows.reshape(piece_rows.shape[0], 3 * channels)
    projected = jnp.dot(features, flat_piece, preferred_element_type=jnp.float32)
    projected = projected.astype(jnp.bfloat16).reshape(tok_rows, 3, channels)
    rim_rows = shifted(projected[tok_rows - 2 :], "seq", 1)
    extended = jnp.concatenate([rim_rows, projected], axis=0).astype(jnp.float32)
    mixed_in = (
        short_filter[0] * extended[2:]
        + short_filter[1] * extended[1:-1]
        + short_filter[2] * extended[:-2]
    )
    query_gate = mixed_in[:, 0]
    product = (mixed_in[:, 1] * mixed_in[:, 2]).astype(jnp.bfloat16)
    local_pos = jnp.arange(tok_rows, dtype=jnp.int32)
    sources = jnp.arange(seq_parts, dtype=jnp.int32)
    within_rows = my_index * group_rows + jnp.arange(group_rows, dtype=jnp.int32)
    block_pos = sources[:, None] * tok_rows + within_rows[None, :]
    block_angle = TWO_PI * block_pos.astype(jnp.float32) / padded_len
    pos_angle = TWO_PI * (my_index * tok_rows + local_pos).astype(jnp.float32) / padded_len
    values = product.astype(jnp.float32)
    state_re = jnp.concatenate([values, values * jnp.cos(pos_angle)[:, None]], -1)
    state_im = jnp.concatenate([jnp.zeros_like(values), -values * jnp.sin(pos_angle)[:, None]], -1)
    state_now = jnp.stack([state_re, state_im])
    for section_bit in range(bit_count - 1, -1, -1):
        half_span = 1 << section_bit
        partner = swapped(state_now.astype(jnp.bfloat16), "seq", section_bit).astype(
            state_now.dtype
        )
        upper_half = my_index >> section_bit & 1 == 1
        phase_now = TWO_PI * (my_index % half_span).astype(jnp.float32) / (2 * half_span)
        difference = partner - state_now
        rot_re = difference[0] * jnp.cos(phase_now) + difference[1] * jnp.sin(phase_now)
        rot_im = difference[1] * jnp.cos(phase_now) - difference[0] * jnp.sin(phase_now)
        state_now = jnp.where(upper_half, jnp.stack([rot_re, rot_im]), state_now + partner)
    own_freq = reversed_bits(my_index, bit_count)
    holders = reversed_bits(sources, bit_count)
    twist_angle = TWO_PI * (local_pos * own_freq % length).astype(jnp.float32) / length
    twist_re = jnp.cos(twist_angle)[:, None]
    twist_im = -jnp.sin(twist_angle)[:, None]
    spec_re = state_now[0] * twist_re - state_now[1] * twist_im
    spec_im = state_now[0] * twist_im + state_now[1] * twist_re
    kernel_table = angle_table(local_pos, local_pos, tok_rows)
    dft_re = jnp.cos(kernel_table)
    dft_im = -jnp.sin(kernel_table)
    spec_re, spec_im = complex_dot(dft_re, dft_im, spec_re, spec_im)
    parity = (jnp.arange(2 * channels, dtype=jnp.int32) >= channels).astype(jnp.int32)
    full_freq = 2 * (own_freq + seq_parts * local_pos)[:, None] + parity[None, :]
    freq_angle = TWO_PI * full_freq.astype(jnp.float32) / padded_len
    half_sine = jnp.sin(0.5 * freq_angle)
    sine_full = jnp.sin(freq_angle)
    sign_flip = 1.0 - 2.0 * parity.astype(jnp.float32)
    rates_both = jnp.concatenate([decay_rate, decay_rate], -1)
    residues_both = jnp.concatenate([residue, residue], -1)
    filt_re = jnp.zeros_like(spec_re)
    filt_im = jnp.zeros_like(spec_re)
    for mode_index in range(rates_both.shape[0]):
        rate_now = rates_both[mode_index]
        decay_now = jnp.exp(-rate_now)
        numerator = residues_both[mode_index] * (1.0 - sign_flip * jnp.exp(-rate_now * length))
        denom_re = -jnp.expm1(-rate_now) + 2.0 * decay_now * half_sine * half_sine
        denom_im = decay_now * sine_full
        scaled = numerator / (denom_re * denom_re + denom_im * denom_im)
        filt_re = filt_re + scaled * denom_re
        filt_im = filt_im - scaled * denom_im
    prod_re = spec_re * filt_re - spec_im * filt_im
    prod_im = spec_re * filt_im + spec_im * filt_re
    inv_re, inv_im = complex_dot(dft_re, -dft_im, prod_re, prod_im)
    back_re = inv_re * twist_re + inv_im * twist_im
    back_im = inv_im * twist_re - inv_re * twist_im
    returned = lax.all_to_all(
        jnp.stack([back_re, back_im]).reshape(2, 1, tok_rows, 2 * channels).astype(jnp.bfloat16),
        "seq",
        split_axis=2,
        concat_axis=1,
        tiled=True,
    ).astype(jnp.float32)
    inverse_angle = angle_table(sources, holders, seq_parts)
    block_re, block_im = complex_mix(
        jnp.cos(inverse_angle), jnp.sin(inverse_angle), returned[0], returned[1]
    )
    conv_blocks = (
        block_re[..., :channels]
        + jnp.cos(block_angle)[:, :, None] * block_re[..., channels:]
        - jnp.sin(block_angle)[:, :, None] * block_im[..., channels:]
    )
    conv_blocks = conv_blocks / padded_len
    conv_rows = lax.all_to_all(conv_blocks, "seq", split_axis=0, concat_axis=1, tiled=True)[0]
    mixed_out = (query_gate * (conv_rows + skip * product.astype(jnp.float32))).astype(jnp.bfloat16)
    return mixed_out


MESH = pl.DeviceIdType.MESH
PIECES = 8
AHEAD = 2
RELAY = 3
BEHIND = 3
EARLY = 2
SEGMENTS = 8


def fused_block(
    ids_ref, residual_ref, table_ref, w_ref, taps_ref, rate_ref, residue_ref, skip_ref, out_ref,
    x_ref, residual, table, held, weights, stage, outbox, inbox, edge, halo, proj, values, conv, enter, ends, states,
    in_sem, load_sem, wide_send, wide_recv, weight_send, weight_recv, x_send, x_recv, via_send, via_recv,
    box_send, box_recv, edge_send, edge_recv, end_send, end_recv,
):
    y = lax.axis_index("grp")
    z = lax.axis_index("seq")
    ch = lax.axis_index("ch")
    sub = lax.axis_index("sub")
    rows = x_ref.shape[0]
    width = x_ref.shape[1]
    parts, tall = 4, width // 2
    units, lanes = weights.shape[1], weights.shape[3]
    blocks = units // 3
    pairs = 2 * blocks
    modes = rate_ref.shape[0]
    taps_count = taps_ref.shape[0]
    span = rows // SEGMENTS
    f32, bf16 = jnp.float32, jnp.bfloat16

    side = z // 2
    near = 1 + side
    outer = 3 * side
    far_near = 2 - side
    far_outer = 3 - outer
    is_outer = z == outer
    is_inner = z == near
    mine = lax.rem(z, 2)
    across = {"ch": 1 - ch}
    sibling = {"sub": 1 - sub}
    other_group = {"grp": 1 - y}

    def remote(src, dst, send, recv, device):
        return pltpu.make_async_remote_copy(
            src_ref=src, dst_ref=dst, send_sem=send, recv_sem=recv, device_id=device, device_id_type=MESH
        )

    def place(u):
        pair = u < pairs
        return jnp.where(pair, 1 + lax.rem(u, 2), 0), jnp.where(pair, u // 2, u - pairs)

    def load(u):
        g, h = (1 + u % 2, u // 2) if u < pairs else (0, u - pairs)
        return pltpu.make_async_copy(
            w_ref.at[g, :, pl.ds(h * lanes, lanes)], weights.at[mine, u], load_sem.at[u]
        )

    def loaded(u):
        pltpu.make_async_copy(w_ref.at[0, :, pl.ds(0, lanes)], weights.at[mine, u], load_sem.at[u]).wait()

    fetch = [
        pltpu.make_async_copy(table_ref, table, in_sem.at[0]),
        pltpu.make_async_copy(residual_ref, residual, in_sem.at[1]),
    ]

    @pl.when(is_outer)
    def _():
        load(0).start()

    for copy in fetch:
        copy.start()

    @pl.when(is_inner)
    def _():
        load(0).start()

    for u in range(1, units):
        load(u).start()
    halo[...] = jnp.zeros_like(halo)
    states[...] = jnp.zeros_like(states)

    barrier = pltpu.get_barrier_semaphore()
    for device in (across, sibling, other_group):
        pl.semaphore_signal(barrier, inc=1, device_id=device, device_id_type=MESH)
    for apart in range(1, parts):
        pl.semaphore_signal(barrier, inc=1, device_id={"seq": lax.rem(z + apart, parts)}, device_id_type=MESH)
    pl.semaphore_wait(barrier, 3 + parts - 1)

    share = pl.ds(pl.multiple_of(y * tall, tall), tall)

    def weight_up(u):
        at = weights.at[mine, u, share]
        return remote(at, at, weight_send.at[u], weight_recv.at[u], {"seq": near})

    def weight_wide(u):
        at = weights.at[1 - mine, u, share]
        return remote(at, at, wide_send.at[u], wide_recv.at[u], other_group)

    def weight_share(u):
        at = weights.at[1 - mine, u, share]
        remote(at, at, weight_send.at[u], weight_recv.at[u], other_group).wait_recv()
        weight_wide(u).start()

    def prepare():
        for copy in fetch:
            copy.wait()
        vocab = lax.broadcasted_iota(jnp.int32, (table.shape[0], rows), 0)
        onehot = (vocab == ids_ref[...]).astype(f32).astype(bf16)
        embedded = lax.dot_general(onehot, table[...], (((0,), (0,)), ((), ())), preferred_element_type=f32)
        x_ref[...] = (residual[...].astype(f32) + embedded).astype(bf16)

    step = rows // PIECES
    direct = PIECES // 2

    def piece(p):
        return pl.ds(p * step, step) if isinstance(p, int) else pl.ds(pl.multiple_of(p * step, step), step)

    def target(c):
        f = 2 * c + sub
        return jnp.where((f == z) & is_outer, z, 1 + c)

    goal = target(ch)
    relay_goal = target(1 - ch)
    stays = goal == z
    relay_stays = relay_goal == z

    def own_direct(p):
        return remote(x_ref.at[piece(p)], held.at[z, sub, piece(p)], x_send.at[0, p], x_recv.at[z, sub, p], {"seq": goal})

    def own_local(p):
        return pltpu.make_async_copy(x_ref.at[piece(p)], held.at[z, sub, piece(p)], x_recv.at[z, sub, p])

    def own_across(p):
        return remote(x_ref.at[piece(p)], held.at[z, sub, piece(p)], x_send.at[0, p], x_recv.at[z, sub, p], across)

    def own_via(p):
        return remote(x_ref.at[piece(p)], stage.at[p - direct], x_send.at[0, p], via_recv.at[p - direct], across)

    def relay(p):
        return remote(
            stage.at[p - direct], held.at[z, sub, piece(p)], via_send.at[p - direct], x_recv.at[z, sub, p],
            {"seq": relay_goal},
        )

    def own_sibling(p):
        return remote(
            x_ref.at[piece(p)], held.at[z, sub, piece(p)], x_send.at[1 + parts + z, p], x_recv.at[z, sub, p], sibling
        )

    def own_first():
        @pl.when(stays)
        def _():
            for p in range(direct):
                own_across(p).start()
            for p in range(PIECES):
                own_local(p).start()
                own_sibling(p).start()

    def own_rest():
        @pl.when(stays)
        def _():
            for p in range(direct, PIECES):
                own_across(p).start()

    def send_via():
        @pl.when(jnp.logical_not(stays))
        def _():
            for p in range(direct, PIECES):
                own_via(p).start()

    def send_direct():
        @pl.when(jnp.logical_not(stays))
        def _():
            for p in range(direct):
                own_direct(p).start()

    def send_relay():
        @pl.when(jnp.logical_not(relay_stays))
        def _():
            for p in range(direct, PIECES):
                own_via(p).wait_recv()
                relay(p).start()

    at_home = ch == side
    first = jnp.where(at_home, 0, direct)
    second = direct - first

    def arrived(t, s, p):
        at = held.at[t, s, piece(p)]
        remote(at, at, x_send.at[1, p], x_recv.at[t, s, p], across).wait_recv()

    def to_across(t, p):
        at = held.at[t, sub, piece(p)]
        return remote(at, at, x_send.at[1 + t, p], x_recv.at[t, sub, p], across)

    def to_sibling(t, p):
        at = held.at[t, sub, piece(p)]
        return remote(at, at, x_send.at[1 + parts + t, p], x_recv.at[t, sub, p], sibling)

    def primary(t):
        for n in range(direct):
            p = first + n
            arrived(t, sub, p)
            to_across(t, p).start()
            to_sibling(t, p).start()

    def secondary(t):
        for n in range(PIECES - direct):
            p = second + n
            arrived(t, sub, p)
            to_sibling(t, p).start()

    def own_block():
        for p in range(PIECES):
            arrived(z, sub, p)

            @pl.when(jnp.logical_not(at_home))
            def _():
                to_sibling(z, p).start()

    def from_sibling(t):
        for p in range(PIECES):
            arrived(t, 1 - sub, p)

    def outgoing(kind, u, device, there):
        return remote(
            outbox.at[kind, u], inbox.at[there, u], box_send.at[kind, u], box_recv.at[there, u], device
        )

    def both(t, u):
        return jnp.dot(held[t, 0], weights[0, u], preferred_element_type=f32) + jnp.dot(
            held[t, 1], weights[1, u], preferred_element_type=f32
        )

    def one(t, u):
        return jnp.dot(held[t, mine], weights[mine, u], preferred_element_type=f32)

    def received(kind, u):
        outgoing(kind, u, across, kind).wait_recv()
        return inbox[kind, u].astype(f32)

    def far(kind, t, u):
        outbox[kind, u] = both(t, u).astype(bf16)
        outgoing(kind, u, {"seq": far_near}, kind).start()

    def weights_ready(u):
        loaded(u)
        at = weights.at[1 - mine, u, share]
        remote(at, at, wide_send.at[u], wide_recv.at[u], other_group).wait_recv()

    def to_outer(u):
        acc = one(outer, u)
        outbox[2, u] = (acc + received(1, u)).astype(bf16)
        outgoing(2, u, {"seq": outer}, 0).start()

    def edge_copy(u):
        return remote(edge.at[u], halo.at[u], edge_send.at[u], edge_recv.at[u], {"seq": z + 1})

    def finished(acc, u):
        total = (acc + received(0, u)).astype(bf16)
        proj[u, SEGMENTS:, :] = total.astype(f32)

        @pl.when(z < parts - 1)
        def _():
            edge[u] = total[rows - 16 :]
            edge_copy(u).start()

    def lanes_at(h):
        return pl.ds(pl.multiple_of(h * lanes, lanes), lanes)

    def mixed(g, u, h):
        proj[u, :SEGMENTS, :] = halo[u].astype(f32)[16 - SEGMENTS :]
        acc = None
        for i in range(taps_count):
            term = taps_ref[i, g : g + 1, lanes_at(h)] * proj[u, pl.ds(SEGMENTS - i, rows), :]
            acc = term if acc is None else acc + term
        return acc

    def halo_ready(u):
        @pl.when(z > 0)
        def _():
            remote(edge.at[u], halo.at[u], edge_send.at[u], edge_recv.at[u], across).wait_recv()

    index = lax.broadcasted_iota(jnp.int32, (SEGMENTS, lanes), 0)

    def wide(row):
        return jnp.broadcast_to(row, (SEGMENTS, lanes))

    def end_copy(h, apart):
        return remote(
            ends.at[h], states.at[z, h], end_send.at[apart - 1, h], end_recv.at[z, h], {"seq": z + apart}
        )

    def local_scan(h):
        rates = rate_ref[:, lanes_at(h)]
        decay = [wide(jnp.exp(-rates[m : m + 1, :])) for m in range(modes)]
        zero = jnp.zeros((SEGMENTS, lanes), f32)

        def advance(j, state):
            now = values[h, pl.ds(j, SEGMENTS, stride=span), :]
            return tuple(v * d + now for v, d in zip(state, decay))

        state = lax.fori_loop(0, span, advance, (zero,) * modes, unroll=4)

        def down(v, by):
            return jnp.where(index >= by, pltpu.roll(v, by, 0), 0.0)

        for m in range(modes):
            carry = down(state[m], 1)
            by = 1
            while by < SEGMENTS:
                carry = carry + jnp.exp(-rates[m : m + 1, :] * (span * by)) * down(carry, by)
                by *= 2
            enter[h, m] = carry
            last = slice(SEGMENTS - 1, SEGMENTS)
            ends[h, m : m + 1, :] = jnp.exp(-rates[m : m + 1, :] * span) * carry[last] + state[m][last]
        for apart in range(1, parts):
            @pl.when(z + apart < parts)
            def _():
                end_copy(h, apart).start()

    def full_scan(h):
        rates = rate_ref[:, lanes_at(h)]
        scale = residue_ref[:, lanes_at(h)]
        for t in range(parts - 1):
            @pl.when(t < z)
            def _():
                remote(ends.at[h], states.at[t, h], end_send.at[0, h], end_recv.at[t, h], across).wait_recv()

        decay = [wide(jnp.exp(-rates[m : m + 1, :])) for m in range(modes)]
        weight = [wide(scale[m : m + 1, :]) for m in range(modes)]
        whole = jnp.exp(-rates * rows)
        start = states[0, h]
        for t in range(1, parts - 1):
            start = jnp.where(t < z, start * whole + states[t, h], start)
        steps = (index * span).astype(f32)
        begin = tuple(
            enter[h, m] + jnp.exp(-rates[m : m + 1, :] * steps) * start[m : m + 1, :] for m in range(modes)
        )
        skips = wide(skip_ref[:, lanes_at(h)])

        def advance(j, state):
            here = pl.ds(j, SEGMENTS, stride=span)
            now = values[h, here, :]
            state = tuple(v * d + now for v, d in zip(state, decay))
            terms = [v * w for v, w in zip(state, weight)] + [skips * now]
            while len(terms) > 1:
                terms = [a + b for a, b in zip(terms[::2], terms[1::2])] + terms[len(terms) // 2 * 2 :]
            conv[h, here, :] = terms[0]
            return state

        lax.fori_loop(0, span, advance, begin, unroll=4)

    def mix(u):
        halo_ready(u)
        _, h = place(u)

        @pl.when((u < pairs) & (lax.rem(u, 2) == 1))
        def _():
            product = mixed(1, u - 1, h) * mixed(2, u, h)
            values[h] = product.astype(bf16).astype(f32)
            local_scan(h)

        @pl.when(u >= pairs)
        def _():
            out_ref[:, lanes_at(h)] = (mixed(0, u, h) * conv[h]).astype(out_ref.dtype)

    @pl.when(is_outer)
    def _():
        for u in range(EARLY):
            loaded(u)
            weight_up(u).start()
        prepare()
        send_via()
        own_first()
        own_rest()
        send_direct()
        send_relay()
        for u in range(EARLY, units):
            loaded(u)
            weight_up(u).start()

        @pl.when(sub == mine)
        def _():
            own_block()

        @pl.when(sub != mine)
        def _():
            from_sibling(z)

        @pl.loop(0, units + 1)
        def _(u):
            @pl.when(u > pairs)
            def _():
                full_scan(u - 1 - pairs)

            @pl.when(u < units)
            def _():
                finished(one(z, u), u)

            @pl.when(u > 0)
            def _():
                mix(u - 1)

    @pl.when(is_inner)
    def _():
        handles_near = sub == mine
        prepare()
        send_via()
        own_first()
        send_direct()
        send_relay()
        weight_share(0)
        primary(far_near)
        weight_share(1)
        secondary(far_near)
        primary(far_outer)
        for u in range(2, AHEAD + RELAY - 1):
            weight_share(u)
        from_sibling(far_near)

        @pl.loop(0, AHEAD)
        def _(u):
            weights_ready(u)
            far(0, far_near, u)

        secondary(far_outer)
        own_rest()
        weight_share(AHEAD + RELAY - 1)

        @pl.when(handles_near)
        def _():
            primary(outer)

        from_sibling(far_outer)
        lag = BEHIND + 2

        @pl.loop(0, units + lag)
        def _(i):
            @pl.when(i < units)
            def _():
                far(1, far_outer, i)

            @pl.when(i + AHEAD < units)
            def _():
                weights_ready(i + AHEAD)
                far(0, far_near, i + AHEAD)

            @pl.when(i + AHEAD + RELAY < units)
            def _():
                weight_share(i + AHEAD + RELAY)

            @pl.when(i == BEHIND - 1)
            def _():
                own_block()

                @pl.when(handles_near)
                def _():
                    secondary(outer)

                from_sibling(z)

                @pl.when(jnp.logical_not(handles_near))
                def _():
                    from_sibling(outer)

            @pl.when((i >= BEHIND) & (i < units + BEHIND))
            def _():
                to_outer(i - BEHIND)
                finished(both(z, i - BEHIND), i - BEHIND)

            @pl.when((i >= pairs + lag - 1) & (i < units + lag - 1))
            def _():
                full_scan(i - pairs - lag + 1)

            @pl.when(i >= lag)
            def _():
                mix(i - lag)

    for p in range(PIECES):
        own_direct(p).wait_send()

    @pl.when(jnp.logical_not(relay_stays))
    def _():
        for p in range(direct, PIECES):
            relay(p).wait_send()

    def own_sent():
        for p in range(PIECES):
            to_sibling(z, p).wait_send()

    def sent(t):
        for n in range(direct):
            to_across(t, first + n).wait_send()
        for p in range(PIECES):
            to_sibling(t, p).wait_send()

    @pl.when(is_outer & (sub == mine))
    def _():
        own_sent()

    @pl.when(is_inner)
    def _():
        sent(far_near)
        sent(far_outer)
        own_sent()

        @pl.when(sub == mine)
        def _():
            sent(outer)

    @pl.loop(0, units)
    def _(u):
        @pl.when(is_outer)
        def _():
            weight_up(u).wait_send()

        @pl.when(is_inner)
        def _():
            weight_wide(u).wait_send()
            for kind in range(3):
                outgoing(kind, u, across, 0).wait_send()

        @pl.when(z < parts - 1)
        def _():
            remote(edge.at[u], halo.at[u], edge_send.at[u], edge_recv.at[u], across).wait_send()

    for h in range(blocks):
        for apart in range(1, parts):
            @pl.when(z + apart < parts)
            def _():
                remote(
                    ends.at[h], states.at[0, h], end_send.at[apart - 1, h], end_recv.at[0, h], across
                ).wait_send()


def fused(token_ids, residual_in, embedding, weight, short_filter, decay_rate, residue, skip):
    rows, width = residual_in.shape
    groups, _, channels = weight.shape
    parts = 4
    modes = decay_rate.shape[0]
    lanes = 128
    blocks = channels // lanes
    units = groups * blocks
    dma = pltpu.SemaphoreType.DMA
    f32, bf16 = jnp.float32, jnp.bfloat16
    vmem = pl.BlockSpec(memory_space=pltpu.VMEM)
    return pl.pallas_call(
        fused_block,
        out_shape=jax.ShapeDtypeStruct((rows, channels), f32),
        in_specs=[vmem] + [pl.BlockSpec(memory_space=pl.ANY)] * 3 + [vmem] * 4,
        out_specs=vmem,
        scratch_shapes=[
            pltpu.VMEM((rows, width), bf16),
            pltpu.VMEM((rows, width), bf16),
            pltpu.VMEM(embedding.shape, bf16),
            pltpu.VMEM((parts, 2, rows, width), bf16),
            pltpu.VMEM((2, units, width, lanes), bf16),
            pltpu.VMEM((PIECES - PIECES // 2, rows // PIECES, width), bf16),
            pltpu.VMEM((3, units, rows, lanes), bf16),
            pltpu.VMEM((2, units, rows, lanes), bf16),
            pltpu.VMEM((units, 16, lanes), bf16),
            pltpu.VMEM((units, 16, lanes), bf16),
            pltpu.VMEM((units, rows + SEGMENTS, lanes), f32),
            pltpu.VMEM((blocks, rows, lanes), f32),
            pltpu.VMEM((blocks, rows, lanes), f32),
            pltpu.VMEM((blocks, modes, SEGMENTS, lanes), f32),
            pltpu.VMEM((blocks, modes, lanes), f32),
            pltpu.VMEM((parts - 1, blocks, modes, lanes), f32),
            dma((2,)),
            dma((units,)),
            dma((units,)),
            dma((units,)),
            dma((units,)),
            dma((units,)),
            dma((1 + 2 * parts, PIECES)),
            dma((parts, 2, PIECES)),
            dma((PIECES - PIECES // 2,)),
            dma((PIECES - PIECES // 2,)),
            dma((3, units)),
            dma((2, units)),
            dma((units,)),
            dma((units,)),
            dma((parts - 1, blocks)),
            dma((parts - 1, blocks)),
        ],
        compiler_params=pltpu.CompilerParams(
            collective_id=0, has_side_effects=True, vmem_limit_bytes=60 * 2**20
        ),
    )(token_ids.reshape(1, -1), residual_in, embedding, weight, short_filter, decay_rate, residue, skip.reshape(1, -1))


def fast_shards(token_ids, residual_in, embedding, in_weight, short_filter, decay_rate, residue, skip):
    weight = in_weight.transpose(1, 0, 2)
    mixed = fused(token_ids, residual_in, embedding, weight, short_filter, decay_rate, residue, skip)
    return mixed.astype(jnp.bfloat16)


def fits(mesh):
    shape = mesh.shape
    return shape["seq"] == 4 and shape["grp"] == 2 and shape["ch"] == 2 and shape["sub"] == 2


def solution(mesh):
    return jax.shard_map(
        fast_shards if fits(mesh) else shards,
        mesh=mesh,
        in_specs=(
            P(("grp", "seq")),
            P(("grp", "seq"), ("ch", "sub")),
            P(None, ("ch", "sub")),
            P("seq", None, ("ch", "sub")),
            P(None, None, ("ch", "sub")),
            P(None, ("ch", "sub")),
            P(None, ("ch", "sub")),
            P(("ch", "sub")),
        ),
        out_specs=P(("grp", "seq"), ("ch", "sub")),
        check_vma=False,
    )
```
